32 devices in a mesh: gx: 4 (over z), gy: 2 (over y), gz: 4 (over x, core).
Axes of the slice: x: 2, y: 2, z: 4, core: 2. Of those that a mesh axis runs over, the one named last changes fastest.
Arguments:
- random_vectors: float32 [64, 16, 128, 128], P('gx', 'gy', 'gz'), may hold values from -6 to 6
- potential: float32 [64, 16, 128], P('gx', 'gy', 'gz'), may hold values from -2.5 to 2.5
Outputs:
- moments: float32 [9, 128], replicated
- chebyshev_vector: float32 [64, 16, 128, 128], P('gx', 'gy', 'gz')
The draws below stay inside these ranges and needn't reach their ends.
All inputs are finite; a program needn't handle non-finite values.
Results may differ from the reference program's by a relative error of at most 0.0001.
Values sent between devices are 32-bit elements; how exact they have to be, the bound alone decides.
No kernel may reach another device: no remote copies, remote signals or barrier semaphores. Data moves between devices by JAX's collectives and lax.ppermute only.
A program may use at most 64 MiB of HBM per device.

```python
import math
import jax
import jax.numpy as jnp
from jax import lax

R = 128
ITERS = 4
NX = 64
NY = 16
NZ = 128


def level_of(key, extent, pieces, low, largest):
    factor_of, own = 1.0, jax.random.fold_in(key, 6)
    for dim, parts in pieces:
        heights = jnp.exp(jax.random.uniform(jax.random.fold_in(own, dim), (parts,), jnp.float32, low / len(pieces), largest / len(pieces)))
        factor_of = factor_of * jnp.repeat(heights, extent[dim] // parts).reshape([-1 if axis == dim else 1 for axis in range(len(extent))])
    return factor_of


def bell_draw(own_key, extent, deviation, bound, split=(), held_as=jnp.bfloat16):
    values = deviation * jax.random.normal(own_key, extent, jnp.float32)
    if split:
        values = values * level_of(own_key, extent, split, -0.22, 0.18)
    return jnp.clip(values, -bound, bound).astype(held_as)


def setup_inputs(seed: int = 0) -> dict:
    splits = jax.random.split(jax.random.key(seed), 3)
    random_vectors = bell_draw(splits[0], (NX, NY, NZ, R), 1.0, 6.0, ((0, 4), (1, 2), (2, 4)), jnp.float32)
    potential = jnp.clip(jax.random.uniform(splits[1], (NX, NY, NZ), jnp.float32, -2.5, 2.5) * level_of(splits[1], (NX, NY, NZ), ((0, 4), (1, 2), (2, 4)), -0.4, 0.0), -2.5, 2.5)
    return dict(random_vectors=random_vectors, potential=potential)


def apply_hamiltonian(field, potential):
    beside = jnp.roll(field, 1, 0) + jnp.roll(field, -1, 0)
    beside = beside + jnp.roll(field, 1, 1) + jnp.roll(field, -1, 1)
    beside = beside + jnp.roll(field, 1, 2) + jnp.roll(field, -1, 2)
    return (potential[..., None] * field - beside) / 9.0


def reference(random_vectors, potential):
    width = math.gcd(R, 16)
    groups = R // width

    def one_block(start):
        previous = start
        current = apply_hamiltonian(start, potential)
        sums = [jnp.sum(start * start, axis=(0, 1, 2)), jnp.sum(start * current, axis=(0, 1, 2))]
        keep = current
        for index in range(1, 2 * ITERS):
            following = 2.0 * apply_hamiltonian(current, potential) - previous
            sums.append(jnp.sum(start * following, axis=(0, 1, 2)))
            previous, current = current, following
            if index + 1 == ITERS:
                keep = following
        return jnp.stack(sums), keep

    blocks = jnp.moveaxis(random_vectors.reshape(NX, NY, NZ, groups, width), 3, 0)
    sums, keeps = lax.map(one_block, blocks)
    moments = jnp.moveaxis(sums, 0, 1).reshape(2 * ITERS + 1, R) / (NX * NY * NZ)
    chebyshev_vector = jnp.moveaxis(keeps, 0, 3).reshape(NX, NY, NZ, R)
    return moments, chebyshev_vector
```

```python
import jax
import jax.numpy as jnp
from jax import lax
from jax.sharding import PartitionSpec as P

ITERS = 4


def around(cells, axis, dim):
    count = lax.axis_size(axis)
    size = cells.shape[dim]
    head = lax.slice_in_dim(cells, 0, 1, axis=dim)
    tail = lax.slice_in_dim(cells, size - 1, size, axis=dim)
    if count == 1:
        return tail, head
    if count == 2:
        both = lax.ppermute(jnp.concatenate([tail, head], axis=dim), axis, [(0, 1), (1, 0)])
        return lax.slice_in_dim(both, 0, 1, axis=dim), lax.slice_in_dim(both, 1, 2, axis=dim)
    before = lax.ppermute(tail, axis, [(i, (i + 1) % count) for i in range(count)])
    after = lax.ppermute(head, axis, [((i + 1) % count, i) for i in range(count)])
    return before, after


def neighbours(cells, before, after, dim):
    size = cells.shape[dim]
    down = jnp.concatenate([before, lax.slice_in_dim(cells, 0, size - 1, axis=dim)], axis=dim)
    up = jnp.concatenate([lax.slice_in_dim(cells, 1, size, axis=dim), after], axis=dim)
    return down + up


def sum_everywhere(partial, axes):
    count = 1
    for axis in axes:
        count *= lax.axis_size(axis)
    copies = jnp.broadcast_to(partial[None], (count,) + partial.shape)
    return jnp.sum(lax.all_to_all(copies, axes, 0, 0), axis=0)


def product(left, right):
    return jnp.sum(left * right, axis=(0, 1, 2))


def shards(random_vectors, potential):
    onsite = potential[..., None]

    def apply_hamiltonian(field):
        y = around(field, "gy", 1)
        z = around(field, "gz", 2)
        x = around(field, "gx", 0)
        beside = neighbours(field, *x, 0) + neighbours(field, *y, 1) + neighbours(field, *z, 2)
        return (onsite * field - beside) / 9.0

    axes = ("gx", "gy", "gz")
    sites = random_vectors.shape[0] * random_vectors.shape[1] * random_vectors.shape[2]
    for axis in axes:
        sites *= lax.axis_size(axis)
    terms = [random_vectors, apply_hamiltonian(random_vectors)]
    for _ in range(ITERS - 1):
        terms.append(2.0 * apply_hamiltonian(terms[-1]) - terms[-2])
    sums = [product(terms[n // 2], terms[(n + 1) // 2]) for n in range(2 * ITERS + 1)]
    totals = sum_everywhere(jnp.stack(sums), axes)
    moments = [totals[0], totals[1]]
    for n in range(2, 2 * ITERS + 1):
        moments.append(2.0 * totals[n] - totals[n % 2])
    return (jnp.stack(moments) / sites, terms[ITERS])


def solution(mesh):
    in_specs = (P("gx", "gy", "gz", None), P("gx", "gy", "gz"))
    out_specs = (P(), P("gx", "gy", "gz", None))
    return jax.shard_map(shards, mesh=mesh, in_specs=in_specs, out_specs=out_specs, check_vma=False)
```

```python
import functools

import jax
import jax.numpy as jnp
from jax import lax
from jax.experimental import pallas as pl
from jax.experimental.pallas import tpu as pltpu
from jax.sharding import PartitionSpec as P


ITERS = 4
AXES = ("gx", "gy", "gz")
TILE = 8
LANES = 128
HALF = LANES // 2


def around(cells, axis, dim):
    count = lax.axis_size(axis)
    size = cells.shape[dim]
    head = lax.slice_in_dim(cells, 0, 1, axis=dim)
    tail = lax.slice_in_dim(cells, size - 1, size, axis=dim)
    if count == 1:
        return tail, head
    if count == 2:
        both = lax.ppermute(jnp.concatenate([tail, head], axis=dim), axis, [(0, 1), (1, 0)])
        return lax.slice_in_dim(both, 0, 1, axis=dim), lax.slice_in_dim(both, 1, 2, axis=dim)
    return to_next(tail, axis), to_previous(head, axis)


def neighbours(cells, before, after, dim):
    size = cells.shape[dim]
    down = jnp.concatenate([before, lax.slice_in_dim(cells, 0, size - 1, axis=dim)], axis=dim)
    up = jnp.concatenate([lax.slice_in_dim(cells, 1, size, axis=dim), after], axis=dim)
    return down + up


def to_next(block, axis):
    count = lax.axis_size(axis)
    return lax.ppermute(block, axis, [(i, (i + 1) % count) for i in range(count)])


def to_previous(block, axis):
    count = lax.axis_size(axis)
    return lax.ppermute(block, axis, [((i + 1) % count, i) for i in range(count)])


def swap(block):
    return lax.ppermute(block, "gy", [(0, 1), (1, 0)])


def sum_over(partial, axes):
    count = 1
    for axis in axes:
        count *= lax.axis_size(axis)
    copies = jnp.broadcast_to(partial[None], (count,) + partial.shape)
    return jnp.sum(lax.all_to_all(copies, axes, 0, 0), axis=0)


def moments_of(totals, shape):
    sites = shape[0] * shape[1] * shape[2]
    for axis in AXES:
        sites *= lax.axis_size(axis)
    lower = jnp.where(jnp.arange(totals.shape[0])[:, None] % 2 == 0, totals[0], totals[1])
    first = jnp.arange(totals.shape[0])[:, None] < 2
    return jnp.where(first, totals, 2.0 * totals - lower) / sites


def step_by_step(random_vectors, potential):
    onsite = potential[..., None]

    def apply_hamiltonian(field):
        y = around(field, "gy", 1)
        z = around(field, "gz", 2)
        x = around(field, "gx", 0)
        beside = neighbours(field, *x, 0) + neighbours(field, *y, 1) + neighbours(field, *z, 2)
        return (onsite * field - beside) / 9.0

    terms = [random_vectors, apply_hamiltonian(random_vectors)]
    for _ in range(ITERS - 1):
        terms.append(2.0 * apply_hamiltonian(terms[-1]) - terms[-2])
    sums = [jnp.sum(terms[n // 2] * terms[(n + 1) // 2], axis=(0, 1, 2)) for n in range(2 * ITERS + 1)]
    return moments_of(sum_over(jnp.stack(sums), AXES), random_vectors.shape), terms[ITERS]


VM = pl.BlockSpec(memory_space=pltpu.VMEM)
SM = pl.BlockSpec(memory_space=pltpu.SMEM)


def call(body, outs, scratch=(), n_in=0, cost=0, limit=8):
    run = pl.pallas_call(
        body,
        out_shape=outs,
        in_specs=[SM] + [VM] * n_in,
        out_specs=jax.tree.map(lambda out: VM if isinstance(out, type(f32(1))) else pl.BlockSpec(memory_space=pl.ANY), outs),
        scratch_shapes=list(scratch),
        cost_estimate=pl.CostEstimate(flops=cost, bytes_accessed=cost, transcendentals=0),
        compiler_params=pltpu.CompilerParams(vmem_limit_bytes=limit * 1024 * 1024),
    )

    def held(place, *blocks):
        return run(place, *(pltpu.with_memory_space_constraint(block, pltpu.VMEM) for block in blocks))

    return held


def f32(*shape):
    return pltpu.VMEM(shape, jnp.float32)


def other_half(place):
    lane = lax.broadcasted_iota(jnp.int32, (TILE, LANES), 1)
    return (lane >= HALF) != (place == 1)


def tile_rows(place, pair, tiles, kept):
    mirror = tiles - 1 - 2 * pair
    which = (1 - place) if kept else place
    return pl.ds(pl.multiple_of((pair + which * mirror) * TILE, TILE), TILE)


def rolled(tile):
    return pltpu.roll(tile, HALF, axis=tile.ndim - 1)


def pack_tile(place, other, src, x, y, pair, tiles):
    kept = src[x, y, tile_rows(place, pair, tiles, True), :]
    moved = src[x, y, tile_rows(place, pair, tiles, False), :]
    return jnp.where(other, kept, rolled(moved))


def merge_tiles(place, other, pay, own, own_x, x, y, slot, pair, tiles, write):
    got = pay[x, y, slot * TILE : (slot + 1) * TILE, :]
    kept = tile_rows(place, pair, tiles, True)
    moved = tile_rows(place, pair, tiles, False)
    write(kept, jnp.where(other, got, own[own_x, y, kept, :]))
    write(moved, jnp.where(other, rolled(got), own[own_x, y, moved, :]))


def pack_kernel(pairs, tiles, place_ref, src, *outs):
    place = place_ref[0]
    other = other_half(place)

    @pl.loop(0, src.shape[0])
    def _(x):
        for y in range(src.shape[1]):
            for out, which in zip(outs, pairs):
                for slot, pair in enumerate(which):
                    out[x, y, slot * TILE : (slot + 1) * TILE, :] = pack_tile(place, other, src, x, y, pair, tiles)


def face_kernel(tiles, place_ref, own, pay, out, z_next, z_previous):
    place = place_ref[0]
    other = other_half(place)

    @pl.loop(0, out.shape[0])
    def _(x):
        for y in range(out.shape[1]):
            for pair in range(tiles // 2):

                def write(rows, tile, y=y):
                    out[x, y, rows, :] = tile

                merge_tiles(place, other, pay, own, x, x, y, pair, pair, tiles, write)
        low = lax.broadcasted_iota(jnp.int32, (TILE, LANES), 0) < TILE // 2
        half = out.shape[1] // 2
        for y in range(half):
            head = [out[x, w, 0:TILE, :] for w in (y, y + half)]
            tail = [out[x, w, (tiles - 1) * TILE : tiles * TILE, :] for w in (y, y + half)]
            z_previous[x, y] = jnp.where(low, head[0], pltpu.roll(head[1], TILE // 2, axis=0))
            z_next[x, y] = jnp.where(low, pltpu.roll(tail[0], TILE // 2, axis=0), tail[1])


def ends_kernel(tiles, place_ref, own, pay, z_next, z_previous):
    place = place_ref[0]
    other = other_half(place)
    half = own.shape[1] // 2

    @pl.loop(0, z_next.shape[0])
    def _(x):
        low = lax.broadcasted_iota(jnp.int32, (TILE, LANES), 0) < TILE // 2

        def end_tiles(y):
            got = pay[x, y]
            turned = rolled(got)
            head_got = jnp.where(place == 1, got, turned)
            tail_got = jnp.where(place == 1, turned, got)
            head = jnp.where(other, head_got, own[x, y, 0:TILE, :])
            tail = jnp.where(other, tail_got, own[x, y, (tiles - 1) * TILE : tiles * TILE, :])
            return head, tail

        for y in range(half):
            a, b = end_tiles(y), end_tiles(y + half)
            z_previous[x, y] = jnp.where(low, a[0], pltpu.roll(b[0], TILE // 2, axis=0))
            z_next[x, y] = jnp.where(low, pltpu.roll(a[1], TILE // 2, axis=0), b[1])


def halo_tiles(low, above, below, x, y):
    up, down = above[x, y], below[x, y]
    return (
        jnp.where(low, up, pltpu.roll(down, TILE // 2, axis=0)),
        jnp.where(low, pltpu.roll(up, TILE // 2, axis=0), down),
    )


def halo_kernel(place_ref, above, below, out):
    half = above.shape[1]

    @pl.loop(0, out.shape[0])
    def _(x):
        low = lax.broadcasted_iota(jnp.int32, (TILE, LANES), 0) < TILE // 2
        for y in range(half):
            out[x, y], out[x, y + half] = halo_tiles(low, above, below, x, y)


def fold(value):
    total = value[0:TILE]
    for start in range(TILE, value.shape[0], TILE):
        total = total + value[start : start + TILE]
    return total


def sweep(level, lo, hi, cur, prev, onsite, out, own_rows, sums=None):
    width = out[0].shape[2]
    rows = out[0].shape[1]

    def row(x, carry):
        carry = list(carry)
        here = [None] * rows

        def at(y):
            if here[y] is None:
                here[y] = cur[0][cur[1] + x, y]
            return here[y]

        for y in range(rows):
            center = at(y)
            below = at(y - 1) if y > 0 else rolled(at(rows - 1))
            above = at(y + 1) if y < rows - 1 else rolled(at(0))
            beside = cur[0][cur[1] + x - 1, y] + cur[0][cur[1] + x + 1, y]
            beside = beside + below + above
            length = center.shape[0]
            beside = beside + pltpu.roll(center, 1, axis=0) + pltpu.roll(center, length - 1, axis=0)
            scaled = onsite[0][onsite[1] + x, y] * center - beside
            if level == 1:
                new = scaled * (1.0 / 9.0)
            else:
                new = scaled * (2.0 / 9.0) - prev[0][prev[1] + x, y]
            new = new[0:width]
            out[0][out[1] + x, y] = new
            if sums is not None:
                mine, base = new[0:own_rows], center[0:own_rows]
                if level == 1:
                    carry[0] = carry[0] + fold(base * base)
                carry[-2] = carry[-2] + fold(base * mine)
                carry[-1] = carry[-1] + fold(mine * mine)
        return tuple(carry)

    if sums is None:
        lax.fori_loop(lo, hi, lambda x, c: row(x, ()) or c, 0)
        return
    count = 3 if level == 1 else 2
    zero = jnp.zeros((TILE, LANES), jnp.float32)
    done = lax.fori_loop(lo, hi, row, (zero,) * count)
    for k, value in enumerate(done):
        sums[2 * level - count + 1 + k] += value


def pack_rows(place, other, src, out):
    tiles = src.shape[2] // TILE

    @pl.loop(0, src.shape[0])
    def _(x):
        for y in range(src.shape[1]):
            for pair in range(tiles // 2):
                out[x, y, pair * TILE : (pair + 1) * TILE, :] = pack_tile(place, other, src, x, y, pair, tiles)


def middle_kernel(n_x, deep, tiles, place_ref, own, pay_ends, pay_rest, left, right, halo_left, halo_right, above, below,
                  onsite, t_out, pay_out, edge1, edge2, edge3, sums, t0, t1, t2, t3):
    place = place_ref[0]
    other = other_half(place)
    z = tiles * TILE
    ny = own.shape[1]

    @pl.loop(0, deep)
    def _(x):
        for y in range(ny):
            t0[x, y, 0:z, :] = left[x, y]
            t0[x, y, z : z + TILE, :] = halo_left[x, y]
            t0[n_x - deep + x, y, 0:z, :] = right[x, y]
            t0[n_x - deep + x, y, z : z + TILE, :] = halo_right[x, y]

    @pl.loop(0, n_x - 2 * deep)
    def _(x):
        low = lax.broadcasted_iota(jnp.int32, (TILE, LANES), 0) < TILE // 2
        for y in range(ny):

            def write(rows, tile, y=y):
                t0[deep + x, y, rows, :] = tile

            merge_tiles(place, other, pay_ends, own, x, x, y, 0, 0, tiles, write)
            for pair in range(1, tiles // 2):
                merge_tiles(place, other, pay_rest, own, x, x, y, pair - 1, pair, tiles, write)
        for y in range(ny // 2):
            first, second = halo_tiles(low, above, below, x, y)
            t0[deep + x, y, z : z + TILE, :] = first
            t0[deep + x, y + ny // 2, z : z + TILE, :] = second

    sums[...] = jnp.zeros_like(sums)
    v = (onsite, 0)
    sweep(1, 1, n_x - 1, (t0, 0), None, v, (t1, 0), z, sums)
    sweep(2, 2, n_x - 2, (t1, 0), (t0, 0), v, (t2, 0), z, sums)
    sweep(3, 3, n_x - 3, (t2, 0), (t1, 0), v, (t3, 0), z, sums)
    sweep(4, 4, n_x - 4, (t3, 0), (t2, 0), v, (t_out, -4), z, sums)
    pack_rows(place, other, t_out, pay_out)
    for edge, ref, low_x in ((edge1, t1, 1), (edge2, t2, 2), (edge3, t3, 3)):
        for k, x in enumerate((low_x, low_x + 1, n_x - 2 - low_x, n_x - 1 - low_x)):
            for y in range(ny):
                edge[k, y] = ref[x, y]


def side_kernel(n_x, deep, tiles, is_left, place_ref, face, halo, face_out, halo_out, edge1, edge2, edge3, onsite, onsite_out, t_out,
                pay_out, sums, t0, t1, t2, t3):
    place = place_ref[0]
    other = other_half(place)
    z = tiles * TILE
    ny = face.shape[1]
    for y in range(ny):
        for k in range(2):
            own_row = k if is_left else deep - 2 + k
            row = deep + k if is_left else k
            t0[row, y, 0:z, :] = face[own_row, y]
            t0[row, y, z : z + TILE, :] = halo[own_row, y]
        for k in range(deep):
            row = k if is_left else 2 + k
            t0[row, y, 0:z, :] = face_out[k, y]
            inner = k - 1 if is_left else k
            if 0 <= inner < deep - 1:
                t0[row, y, z : z + TILE, :] = halo_out[inner, y]
            else:
                t0[row, y, z : z + TILE, :] = jnp.zeros((TILE, LANES), jnp.float32)
        for n, (edge, ref) in enumerate(((edge1, t1), (edge2, t2), (edge3, t3))):
            for k in range(2):
                ref[(deep + n + 1 + k) if is_left else k, y] = edge[k if is_left else 2 + k, y]
    sums[...] = jnp.zeros_like(sums)
    inside, outside = (onsite, 0), (onsite_out, deep if is_left else -n_x)
    if is_left:
        zero0 = zero1 = zero2 = zero3 = deep
    else:
        zero0 = -(n_x - 2)
        zero1, zero2, zero3 = -(n_x - 3), -(n_x - 4), -(n_x - 5)
    refs = ((t0, zero0), (t1, zero1), (t2, zero2), (t3, zero3))
    for level in range(1, ITERS + 1):
        if is_left:
            lo, hi = level - deep, level
            spans = ((lo, 0, None, outside), (0, hi, sums, inside))
            out = (t_out, 0)
        else:
            lo, hi = n_x - level, n_x + deep - level
            spans = ((n_x, hi, None, outside), (lo, n_x, sums, inside))
            out = (t_out, -(n_x - deep))
        if level < ITERS:
            out = refs[level]
        prev = refs[level - 2] if level > 1 else None
        for start, stop, into, v in spans:
            if start < stop:
                sweep(level, start, stop, refs[level - 1], prev, v, out, z, into)
    pack_rows(place, other, t_out, pay_out)


def join_kernel(deep, tiles, place_ref, mid, left, right, pay_mid, pay_left, pay_right, _, whole, out, done):
    place = place_ref[0]
    other = other_half(place)
    n_x = out.shape[0]

    def join(first, count, own, pay):
        @pl.loop(0, count)
        def _(x):
            for y in range(out.shape[1]):
                for pair in range(tiles // 2):

                    def write(rows, tile, y=y):
                        out[first + x, y, rows, :] = tile

                    merge_tiles(place, other, pay, own, x, x, y, pair, pair, tiles, write)
            pltpu.make_async_copy(out.at[first + x], whole.at[first + x], done).start()

    join(deep, n_x - 2 * deep, mid, pay_mid)
    join(0, deep, left, pay_left)
    join(n_x - deep, deep, right, pay_right)
    pltpu.make_async_copy(out, whole, done).wait()


def onsite_rows(potential, place, deep):
    both = jnp.stack([potential, swap(potential)])
    n_x, _, z = potential.shape
    above = to_previous(both[..., : TILE // 2], "gz")
    below = to_next(both[..., z - TILE // 2 :], "gz")
    wide = jnp.concatenate([both, above, below], axis=3)
    before = to_next(wide[:, n_x - deep :], "gx")
    after = to_previous(wide[:, :deep], "gx")
    lane_half = (jnp.arange(LANES) >= HALF).astype(jnp.int32)
    return [jnp.where(lane_half == place, part[0][..., None], part[1][..., None]) for part in (wide, before, after)]


def by_halves(random_vectors, potential):
    n_x, ny, z, _ = random_vectors.shape
    deep = ITERS
    tiles = z // TILE
    wide = z + TILE
    place = lax.axis_index("gy").astype(jnp.int32)
    at = place[None]
    mid = n_x - 2 * deep
    pairs = tuple(range(tiles // 2))

    def packed(raw, *which):
        outs = tuple(f32(raw.shape[0], ny, TILE * len(chosen), LANES) for chosen in which)
        return call(functools.partial(pack_kernel, which, tiles), outs, n_in=1)(at, raw)

    raw_right, raw_left = random_vectors[n_x - deep :], random_vectors[:deep]
    raw_mid = random_vectors[deep : n_x - deep]
    (pay,) = packed(raw_right, pairs)
    got_right = swap(pay)
    (pay,) = packed(raw_left, pairs)
    got_left = swap(pay)
    pay, pay_rest = packed(raw_mid, pairs[:1], pairs[1:])
    got_ends = swap(pay)
    got_rest = swap(pay_rest)

    onsite, onsite_before, onsite_after = onsite_rows(potential, place, deep)

    def face(raw, got):
        outs = (f32(deep, ny, z, LANES), f32(deep, ny // 2, TILE, LANES), f32(deep, ny // 2, TILE, LANES))
        return call(functools.partial(face_kernel, tiles), outs, n_in=2)(at, raw, got)

    right, right_up, right_down = face(raw_right, got_right)
    before = to_next(right, "gx")
    left, left_up, left_down = face(raw_left, got_left)
    after = to_previous(left, "gx")

    left_down, onsite = lax.optimization_barrier((left_down, onsite))
    above = to_previous(jnp.concatenate([left_down, right_down]), "gz")
    below = to_next(jnp.concatenate([left_up, right_up]), "gz")
    halos = call(halo_kernel, f32(2 * deep, ny, TILE, LANES), n_in=2)(at, above, below)
    halo_left, halo_right = halos[:deep], halos[deep:]
    halo_before = to_next(halo_right[1:], "gx")
    halo_after = to_previous(halo_left[:-1], "gx")

    outs = (f32(mid, ny // 2, TILE, LANES), f32(mid, ny // 2, TILE, LANES))
    mid_up, mid_down = call(functools.partial(ends_kernel, tiles), outs, n_in=2)(at, raw_mid, got_ends)
    mid_above = to_previous(mid_down, "gz")
    mid_below = to_next(mid_up, "gz")

    edge = f32(4, ny, wide, LANES)
    n_sums = 2 * ITERS + 1
    sums_shape = f32(n_sums, TILE, LANES)
    deep_row = pltpu.VMEM((n_x, ny, wide, LANES), jnp.float32)
    outs = (f32(mid, ny, z, LANES), f32(mid, ny, z // 2, LANES), edge, edge, edge, sums_shape)
    t_mid, pay_mid, edge1, edge2, edge3, sums_mid = call(
        functools.partial(middle_kernel, n_x, deep, tiles), outs, [deep_row] * 4, n_in=10, limit=24
    )(at, raw_mid, got_ends, got_rest, left, right, halo_left, halo_right, mid_above, mid_below, onsite)
    back_mid = swap(pay_mid)

    side_row = pltpu.VMEM((2 * deep + 1, ny, wide, LANES), jnp.float32)
    outs = (f32(deep, ny, z, LANES), f32(deep, ny, z // 2, LANES), sums_shape)

    def side(is_left, *blocks):
        body = functools.partial(side_kernel, n_x, deep, tiles, is_left)
        return call(body, outs, [side_row] * 4, n_in=9, limit=24)(at, *blocks[:4], edge1, edge2, edge3, onsite, blocks[4])

    t_left, pay_left, sums_left = side(True, left, halo_left, before, halo_before, onsite_before)
    back_left = swap(pay_left)
    t_right, pay_right, sums_right = side(False, right, halo_right, after, halo_after, onsite_after)
    back_right = swap(pay_right)

    sums = jnp.sum(sums_mid + sums_left + sums_right, axis=1)
    sums = sums + jnp.roll(sums, HALF, axis=1)
    upper = jnp.arange(LANES) >= HALF
    sums = sum_over(jnp.where(upper, sums[ITERS:], sums[: ITERS + 1]), ("gx", "gz"))
    both = jnp.stack([sums, swap(sums)])
    turned = jnp.roll(both, HALF, axis=2)
    both = jnp.concatenate([jnp.where(upper, turned, both), jnp.where(upper, both, turned)[:, 1:]], axis=1)
    totals = jnp.where(upper.astype(jnp.int32) == place, both[0], both[1])
    moments = moments_of(totals, random_vectors.shape)

    scratch = [pltpu.VMEM((n_x, ny, z, LANES), jnp.float32), pltpu.SemaphoreType.DMA(())]
    whole = jax.ShapeDtypeStruct((n_x, ny, z, LANES), jnp.float32)
    join = call(functools.partial(join_kernel, deep, tiles), whole, scratch, n_in=7)
    return moments, join(at, t_mid, t_left, t_right, back_mid, back_left, back_right, moments)


def fits(shape):
    n_x, ny, z, lanes = shape
    return (
        lax.axis_size("gy") == 2
        and lax.axis_size("gx") > 1
        and lax.axis_size("gz") > 1
        and lanes == LANES
        and n_x > 2 * ITERS
        and ny % 2 == 0
        and z % (2 * TILE) == 0
        and z >= 4 * TILE
        and ITERS == TILE // 2
    )


def shards(random_vectors, potential):
    if fits(random_vectors.shape):
        return by_halves(random_vectors, potential)
    return step_by_step(random_vectors, potential)


def solution(mesh):
    in_specs = (P("gx", "gy", "gz", None), P("gx", "gy", "gz"))
    out_specs = (P(), P("gx", "gy", "gz", None))
    return jax.shard_map(shards, mesh=mesh, in_specs=in_specs, out_specs=out_specs, check_vma=False)
```
